32 devices in a mesh: tm: 4 (over y, core), tile: 8 (over z, x).
Axes of the slice: x: 2, y: 2, z: 4, core: 2. Of those that a mesh axis runs over, the one named last changes fastest.
Arguments:
- latent: bfloat16 [16, 80, 16, 512], P('tm', 'tile'), may hold values from -120 to 120, as said below
- first_kernel: bfloat16 [3, 3, 3, 512, 512], P(None, None, None, 'tile'), may hold values from -0.0546875 to 0.0546875
- norm_gain: float32 [512], replicated, may hold values from 0.5 to 1.5
- norm_bias: float32 [512], replicated, may hold values from -3 to 3
- second_kernel: bfloat16 [3, 3, 3, 512, 512], P(None, None, None, 'tile'), may hold values from -0.0546875 to 0.0546875
- second_bias: float32 [512], replicated, may hold values from -3 to 3
Outputs:
- decoded: bfloat16 [16, 80, 16, 512], P('tm', 'tile')
The draws below stay inside these ranges and needn't reach their ends.
Inputs may be any that keep to these rules, and one draw needn't show every extreme that they name: Real-valued latent entries.
All inputs are finite; a program needn't handle non-finite values.
Results may differ from the reference program's by a relative error of at most 0.0042.
Values may be sent and summed in bfloat16 or wider, within the bound.
No kernel may reach another device: no remote copies, remote signals or barrier semaphores. Data moves between devices by JAX's collectives and lax.ppermute only.
A program may use at most 192 MiB of HBM per device.

```python
import math
import jax
import jax.numpy as jnp
from jax import lax

C = 512
G = 32
H = 16
NT = 16
W = 80


def draw_latent(key, part):
    noise_key, scale_key = jax.random.split(key, 2)
    shape = (NT, W, H, C)
    channel_scale = jnp.exp(jax.random.uniform(scale_key, (C,), jnp.float32, math.log(0.3), math.log(3.0)))
    frame_pos = jnp.arange(NT, dtype=jnp.float32) / max(NT - 1, 1)
    column_pos = jnp.arange(W, dtype=jnp.float32) / max(W - 1, 1)
    noise = jax.random.truncated_normal(noise_key, -4.0, 4.0, shape, jnp.float32)
    frame_ramp = jnp.exp(math.log(3.0) * frame_pos)
    column_ramp = jnp.exp(math.log(3.0) * column_pos)
    ramp = frame_ramp[:, None, None, None] * column_ramp[None, :, None, None]
    return (noise * ramp * channel_scale).astype(jnp.bfloat16)


def block_scale(rng, extent, cuts, least, largest):
    level, own = 1.0, jax.random.fold_in(rng, 6)
    for dim, shards_of in cuts:
        steps = jnp.exp(jax.random.uniform(jax.random.fold_in(own, dim), (shards_of,), jnp.float32, least / len(cuts), largest / len(cuts)))
        level = level * jnp.repeat(steps, extent[dim] // shards_of).reshape([-1 if axis == dim else 1 for axis in range(len(extent))])
    return level


def scatter_about(own_key, dims, scale, reach, pieces=(), kind=jnp.bfloat16):
    values = jax.random.normal(own_key, dims, jnp.float32) * scale
    if len(pieces) > 0:
        values = block_scale(own_key, dims, pieces, -0.22, 0.18) * values
    return jnp.clip(values, min=-reach, max=reach).astype(kind)


def setup_inputs(seed: int = 0) -> dict:
    key_of = jax.random.split(jax.random.key(seed), 7)
    return {
        "latent": draw_latent(jax.random.fold_in(key_of[6], 71), 0),
        "first_kernel": scatter_about(key_of[1], (3, 3, 3, C, C), (27 * C) ** -0.5, 0.0546875, ((3, 8),)),
        "norm_gain": jnp.clip(jax.random.uniform(key_of[2], (C,), jnp.float32, 0.5, 1.5), 0.5, 1.5),
        "norm_bias": scatter_about(key_of[3], (C,), 0.5, 3.0, (), jnp.float32),
        "second_kernel": scatter_about(key_of[4], (3, 3, 3, C, C), (27 * C) ** -0.5, 0.0546875, ((3, 8),)),
        "second_bias": scatter_about(key_of[5], (C,), 0.5, 3.0, (), jnp.float32),
    }


def causal_conv(field, kernel):
    padded = jnp.pad(field, ((2, 0), (1, 1), (1, 1), (0, 0)))
    frames, columns, rows, chans = field.shape
    total = jnp.zeros((frames * columns * rows, kernel.shape[3]), jnp.float32)
    for a in range(3):
        for b in range(3):
            for c in range(3):
                window = padded[a:a + frames, b:b + columns, c:c + rows].reshape(-1, chans)
                total = total + jnp.dot(window, kernel[a, b, c].T, preferred_element_type=jnp.float32)
    return total.reshape(frames, columns, rows, kernel.shape[3])

def reference(latent, first_kernel, norm_gain, norm_bias, second_kernel, second_bias):
    first = causal_conv(latent, first_kernel)
    grouped = first.reshape(NT, W, H, G, C // G)
    mean = lax.optimization_barrier(jnp.mean(grouped, axis=(0, 1, 2, 4), keepdims=True))
    spread = lax.optimization_barrier(jnp.mean((grouped - mean) ** 2, axis=(0, 1, 2, 4), keepdims=True))
    normed = ((grouped - mean) / jnp.sqrt(spread + 1e-05)).reshape(NT, W, H, C)
    activated = jax.nn.silu(normed * norm_gain + norm_bias).astype(jnp.bfloat16)
    second = causal_conv(activated, second_kernel) + second_bias
    return second.astype(jnp.bfloat16)
```

```python
import functools

import jax
import jax.numpy as jnp
from jax import lax
from jax.experimental import pallas as pl
from jax.experimental.pallas import tpu as pltpu
from jax.sharding import PartitionSpec as P


G = 32
SPLIT = 2
EPS = 1e-05
BF16 = jnp.bfloat16
F32 = jnp.float32


def swap_pair(block):
    count = lax.axis_size("tile")
    return lax.ppermute(block, "tile", [(t, t ^ 1) for t in range(count)])


def shift_strip(block, step):
    count = lax.axis_size("tile")
    move = step * SPLIT
    return lax.ppermute(
        block, "tile", [(t, t + move) for t in range(count) if 0 <= t + move < count]
    )


def after(block, *done):
    return lax.optimization_barrier((block,) + done)[0] if done else block


def gather_weights(kernel, shared, cuts, *done):
    tiles, groups = lax.axis_size("tile"), lax.axis_size("tm")
    ring = tiles // SPLIT
    _, own_outputs, chans = kernel.shape
    place = lax.axis_index("tile") // SPLIT
    if ring != 4 or groups != 4:
        members = [[s + SPLIT * r for r in range(ring)] for s in range(SPLIT)]
        every = lax.all_gather(kernel, "tile", axis_index_groups=members)
        return [(every[r], 0, r, 0) for r in range(ring)], every
    tm = lax.axis_index("tm")
    row, core = tm // 2, tm % 2

    def linear(m, t):
        return m * tiles + t

    along = []
    for m in range(groups):
        for t in range(tiles):
            r, s = divmod(t, SPLIT)
            to = (r + (1 if m % 2 == 0 else ring - 1)) % ring
            along.append((linear(m, t), linear(m, to * SPLIT + s)))
    across = [(m, m ^ 2) for m in range(groups)]
    between = [(m, m ^ 1) for m in range(groups)]
    mine = (place + jnp.where(core == 0, ring - 1, 1)) % ring
    other = (place + jnp.where(core == 0, 1, ring - 1)) % ring
    far = (place + 2) % ring
    width = chans // 2 if shared else chans
    part = width // 2
    low, high = row * (chans // 2), (1 - row) * (chans // 2)
    if not shared:
        low = high = 0
    z1, z2 = [], []
    for first, last in cuts:
        sent = kernel[first:last]
        if shared:
            sent = lax.dynamic_slice(sent, (0, 0, low), (last - first, own_outputs, width))
        z1.append(lax.ppermute(after(sent, *done), ("tm", "tile"), along))
    for k, (first, last) in enumerate(cuts):
        onward = lax.dynamic_slice(
            z1[k], (0, 0, core * part), (last - first, own_outputs, part)
        )
        z2.append(lax.ppermute(onward, ("tm", "tile"), along))
    out = [(kernel, 0, place, 0)]
    for (first, last), near, next_one in zip(cuts, z1, z2):
        for at, value, here, there in (
            (0, near, mine, other),
            (1, next_one, far, far),
        ):
            lane = core * part if at else 0
            lane_other = (1 - core) * part if at else 0
            out.append((value, first, here, low + lane))
            out.append((lax.ppermute(value, "tm", between), first, there, low + lane_other))
            if shared:
                swapped = lax.ppermute(value, "tm", across)
                out.append((swapped, first, here, high + lane))
                out.append((lax.ppermute(swapped, "tm", between), first, there, high + lane_other))
    return out, z2[-1]


def start_weights(refs, firsts, meta, base, w_ref, sems):
    copies = [[], [], []]
    for a in range(3):
        for n, src in enumerate(refs):
            taps, outputs, lanes = src.shape
            low, high = max(9 * a, firsts[n]), min(9 * a + 9, firsts[n] + taps)
            if low >= high:
                continue
            row = pl.multiple_of(meta[base + 2 * n], outputs)
            lane = pl.multiple_of(meta[base + 2 * n + 1], 128)
            copy = pltpu.make_async_copy(
                src.at[low - firsts[n] : high - firsts[n]],
                w_ref.at[low:high, pl.ds(row, outputs), pl.ds(lane, lanes)],
                sems.at[a, n],
            )
            copy.start()
            copies[a].append(copy)
    return copies


def multiply(x_ref, w_ref, acc_ref, frames, cols, rows, a, frame_step):
    size = frame_step * cols * rows

    def body(j, _):
        window = jnp.concatenate(
            [
                x_ref[pl.ds(a + j * frame_step, frame_step), b : b + cols].reshape(
                    size, x_ref.shape[-1]
                )
                for b in range(3)
            ],
            axis=1,
        )
        at = pl.ds(pl.multiple_of(j * size, 16), size)
        for c in range(3):
            part = lax.dot_general(
                window,
                jnp.concatenate([w_ref[(a * 3 + b) * 3 + c] for b in range(3)], axis=1),
                (((1,), (1,)), ((), ())),
                preferred_element_type=F32,
            )
            if a == 0:
                acc_ref[c, at] = part
            else:
                acc_ref[c, at] += part
        return 0

    lax.fori_loop(0, frames // frame_step, body, 0)


def combined(acc_ref, at, rows):
    up, mid, down = acc_ref[0, at], acc_ref[1, at], acc_ref[2, at]
    size = mid.shape[0]
    h = lax.broadcasted_iota(jnp.int32, mid.shape, 0) % rows
    up = jnp.where(h == 0, 0.0, pltpu.roll(up, 1, 0))
    down = jnp.where(h == rows - 1, 0.0, pltpu.roll(down, size - 1, 0))
    return mid + up + down


def conv1_kernel(dims, meta, *refs):
    frames, cols, rows, halo_f, strip, firsts, frame_step = dims
    n_w = len(firsts)
    own, pair, prev, prev_pair, left, right = refs[:6]
    w_refs = refs[6 : 6 + n_w]
    first_ref, sent_ref, stat_ref = refs[6 + n_w : 9 + n_w]
    x_ref, w_ref, acc_ref, x_sems, w_sems = refs[9 + n_w :]
    q = meta[0]
    nf = own.shape[0]
    at_own, at_pair = 2 + q * strip, 2 + (1 - q) * strip
    x_copies = []
    for n, (src, f0, c0, nc) in enumerate(
        (
            (own, nf, at_own, strip),
            (pair, nf, at_pair, strip),
            (prev, 0, at_own, strip),
            (prev_pair, 0, at_pair, strip),
            (left, 0, 0, 2),
            (right, 0, cols, 2),
        )
    ):
        copy = pltpu.make_async_copy(
            src, x_ref.at[f0 : f0 + src.shape[0], pl.ds(c0, nc)], x_sems.at[n]
        )
        copy.start()
        x_copies.append(copy)
    w_copies = start_weights(w_refs, firsts, meta, 1, w_ref, w_sems)
    for copy in x_copies:
        copy.wait()
    for a in range(3):
        for copy in w_copies[a]:
            copy.wait()
        multiply(x_ref, w_ref, acc_ref, frames, cols, rows, a, frame_step)
    line = cols * rows
    width = acc_ref.shape[2]

    def gather(f, total):
        at = pl.ds(pl.multiple_of(f * line, 16), line)
        value = combined(acc_ref, at, rows)
        first_ref[at] = value
        inner = jnp.sum(value[rows : line - rows], axis=0, keepdims=True)
        return total + jnp.where(f >= halo_f, inner, 0.0)

    total = lax.fori_loop(0, frames, gather, jnp.zeros((1, width), F32))
    mean = total / ((frames - halo_f) * (cols - 2) * rows)
    offset = mean.astype(BF16)
    base = offset.astype(F32)

    def centre(f, squares):
        at = pl.ds(pl.multiple_of(f * line, 16), line)
        value = first_ref[at]
        sent_ref[at] = (value - base).astype(BF16)
        away = value[rows : line - rows] - mean
        inner = jnp.sum(away * away, axis=0, keepdims=True)
        return squares + jnp.where(f >= halo_f, inner, 0.0)

    squares = lax.fori_loop(0, frames, centre, jnp.zeros((1, width), F32))
    sent_ref[frames * line :] = jnp.broadcast_to(offset, (16, width))
    stat_ref[...] = jnp.concatenate([mean, squares, jnp.zeros((6, width), F32)], axis=0)


def conv2_kernel(dims, meta, *refs):
    frames, cols, rows, strip, firsts, frame_step = dims
    n_w = len(firsts)
    first_ref, other_ref, norm_ref, bias_ref = refs[:4]
    w_refs = refs[4 : 4 + n_w]
    keep_ref, send_ref = refs[4 + n_w : 6 + n_w]
    x_ref, w_ref, acc_ref, w_sems = refs[6 + n_w :]
    q, has_prev, has_left, has_right = (meta[i] for i in range(4))
    w_copies = start_weights(w_refs, firsts, meta, 4, w_ref, w_sems)
    wide = cols + 2
    line = wide * rows
    width = first_ref.shape[1]
    offset = other_ref[(frames + 2) * line :][:1].astype(F32)

    def activate(f, _):
        at = pl.ds(pl.multiple_of(f * line, 16), line)
        h = lax.broadcasted_iota(jnp.int32, (line, width), 0)
        valid = (
            ((f >= 2) | (has_prev == 1))
            & ((h >= rows) | (has_left == 1))
            & ((h < line - rows) | (has_right == 1))
        )
        for s in range(2):
            lanes = slice(s * width, (s + 1) * width)
            value = first_ref[at] if s == 0 else other_ref[at].astype(F32) + offset
            value = (value - norm_ref[0:1, lanes]) * norm_ref[1:2, lanes] + norm_ref[2:3, lanes]
            value = jnp.where(valid, value / (1.0 + jnp.exp(-value)), 0.0)
            x_ref[f, :, :, lanes] = value.astype(BF16).reshape(wide, rows, width)
        return 0

    lax.fori_loop(0, frames + 2, activate, 0)
    for a in range(3):
        for copy in w_copies[a]:
            copy.wait()
        multiply(x_ref, w_ref, acc_ref, frames, cols, rows, a, frame_step)
    size = strip * rows

    def finish(f, _):
        for ref, s in ((keep_ref, q), (send_ref, 1 - q)):
            at = pl.ds(pl.multiple_of(f * cols * rows + s * size, 16), size)
            value = combined(acc_ref, at, rows) + bias_ref[0:1]
            ref[pl.ds(pl.multiple_of(f * size, 16), size)] = value.astype(BF16)
        return 0

    lax.fori_loop(0, frames, finish, 0)


def merge_kernel(keep_ref, other_ref, order_ref, out_ref):
    half = keep_ref.shape[1]
    nt = (((1,), (1,)), ((), ()))
    out_ref[...] = (
        lax.dot_general(keep_ref[...], order_ref[:, :half], nt, preferred_element_type=F32)
        + lax.dot_general(other_ref[...], order_ref[:, half:], nt, preferred_element_type=F32)
    ).astype(BF16)


ANY = pl.BlockSpec(memory_space=pl.ANY)
VMEM = pl.BlockSpec(memory_space=pltpu.VMEM)
SMEM = pl.BlockSpec(memory_space=pltpu.SMEM)
PARAMS = pltpu.CompilerParams(vmem_limit_bytes=60 * 2**20)


def flatten(weights, own_outputs):
    places = []
    for _, _, piece, lane in weights:
        places += [piece * own_outputs, lane]
    return [w[0] for w in weights], places, tuple(w[1] for w in weights)


def table(values):
    return jnp.stack([jnp.asarray(v, jnp.int32) for v in values])


def conv_cost(positions, chans, outputs):
    flops = 2 * positions * chans * outputs * 27
    return pl.CostEstimate(flops=flops, bytes_accessed=20 * 2**20, transcendentals=0)


def merge_moments(parts, count):
    means = jnp.stack([p[0] for p in parts])
    mean = jnp.mean(means, axis=0)
    squares = sum(p[1] for p in parts) + count * jnp.sum((means - mean) ** 2, axis=0)
    return jnp.stack([mean, squares])


def group_moments(stats, count, size):
    tiles, groups = lax.axis_size("tile"), lax.axis_size("tm")
    ring = tiles // SPLIT
    means = stats[0].reshape(-1, size)
    mean = jnp.mean(means, axis=1)
    squares = jnp.sum(stats[1].reshape(-1, size), axis=1) + count * jnp.sum(
        (means - mean[:, None]) ** 2, axis=1
    )
    own = jnp.stack([mean, squares])
    count = count * size
    parts = [own]
    for s in range(1, ring):
        route = [(t, (t + s * SPLIT) % tiles) for t in range(tiles)]
        parts.append(lax.ppermute(own, "tile", route))
    own = merge_moments(parts, count)
    count = count * ring
    parts = [own]
    for s in range(1, groups):
        route = [(m, (m + s) % groups) for m in range(groups)]
        parts.append(lax.ppermute(own, "tm", route))
    own = merge_moments(parts, count)
    count = count * groups
    both = jnp.concatenate([own, swap_pair(own)], axis=1)
    return jnp.repeat(both[0], size), jnp.repeat(both[1] / count, size)


def shards(latent, first_kernel, norm_gain, norm_bias, second_kernel, second_bias):
    nf, strip, rows, chans = latent.shape
    tiles, groups = lax.axis_size("tile"), lax.axis_size("tm")
    ring = tiles // SPLIT
    own_outputs = first_kernel.shape[3]
    outputs = own_outputs * ring
    tile, tm = lax.axis_index("tile"), lax.axis_index("tm")
    q, place = tile % SPLIT, tile // SPLIT
    wide = strip * SPLIT

    o = jnp.arange(chans)
    parity = jnp.where(o < outputs, q, 1 - q)
    natural = ((o % outputs) // own_outputs * SPLIT + parity) * own_outputs + o % own_outputs
    order = (jnp.arange(chans)[:, None] == natural[None, :]).astype(BF16)

    def ordered(vector):
        pieces = vector.reshape(ring, SPLIT, own_outputs)
        even, odd = pieces[:, 0].reshape(-1), pieces[:, 1].reshape(-1)
        return jnp.where(q == 0, jnp.concatenate([even, odd]), jnp.concatenate([odd, even]))

    w1, through = gather_weights(
        first_kernel.reshape(27, own_outputs, chans), True, ((0, 9), (9, 27))
    )

    prev = lax.ppermute(latent, "tm", [(m, m + 1) for m in range(groups - 1)])
    pair = swap_pair(latent)
    prev_pair = swap_pair(prev)
    both = jnp.concatenate([prev, latent], axis=0)
    both_pair = jnp.concatenate([prev_pair, pair], axis=0)
    last = jnp.where(q == 1, both[:, strip - 2 :], both_pair[:, strip - 2 :])
    start = jnp.where(q == 0, both[:, :2], both_pair[:, :2])
    left = shift_strip(last, 1)
    right = shift_strip(start, -1)

    second = lax.dot_general(
        second_kernel.reshape(27 * own_outputs, chans), order, (((1,), (0,)), ((), ()))
    ).astype(BF16)
    w2, _ = gather_weights(
        second.reshape(27, own_outputs, chans), False, ((0, 27),), through
    )

    halo_f = 2
    f1, c1 = nf + halo_f, wide + 2
    blocks, places, firsts = flatten(w1, own_outputs)
    rows1 = f1 * c1 * rows
    dims = (f1, c1, rows, halo_f, strip, firsts, 2)
    first, sent, stats = pl.pallas_call(
        functools.partial(conv1_kernel, dims),
        out_shape=(
            jax.ShapeDtypeStruct((rows1, outputs), F32),
            jax.ShapeDtypeStruct((rows1 + 16, outputs), BF16),
            jax.ShapeDtypeStruct((8, outputs), F32),
        ),
        in_specs=[SMEM] + [ANY] * (6 + len(blocks)),
        out_specs=(VMEM, VMEM, VMEM),
        scratch_shapes=[
            pltpu.VMEM((2 * nf, wide + 4, rows, chans), BF16),
            pltpu.VMEM((27, outputs, chans), BF16),
            pltpu.VMEM((3, rows1, outputs), F32),
            pltpu.SemaphoreType.DMA((6,)),
            pltpu.SemaphoreType.DMA((3, len(blocks))),
        ],
        compiler_params=PARAMS,
        cost_estimate=conv_cost(rows1, chans, outputs),
        name="conv1",
    )(table([q] + places), latent, pair, prev, prev_pair, left, right, *blocks)

    other = swap_pair(sent)
    mean, spread = group_moments(stats, nf * wide * rows, chans // G)
    norm = jnp.stack(
        [mean, ordered(norm_gain) / jnp.sqrt(spread + EPS), ordered(norm_bias)]
        + [jnp.zeros((chans,), F32)] * 5
    )
    bias = jnp.broadcast_to(ordered(second_bias)[:outputs], (8, outputs))

    blocks, places, firsts = flatten(w2, own_outputs)
    rows2 = nf * wide * rows
    dims = (nf, wide, rows, strip, firsts, 2)
    edges = [q, tm > 0, place > 0, place < ring - 1]
    half = jax.ShapeDtypeStruct((nf * strip * rows, outputs), BF16)
    keep, send = pl.pallas_call(
        functools.partial(conv2_kernel, dims),
        out_shape=(half, half),
        in_specs=[SMEM] + [VMEM] * 4 + [ANY] * len(blocks),
        out_specs=(VMEM, VMEM),
        scratch_shapes=[
            pltpu.VMEM((f1, c1, rows, chans), BF16),
            pltpu.VMEM((27, outputs, chans), BF16),
            pltpu.VMEM((3, rows2, outputs), F32),
            pltpu.SemaphoreType.DMA((3, len(blocks))),
        ],
        compiler_params=PARAMS,
        cost_estimate=conv_cost(rows2, chans, outputs),
        name="conv2",
    )(table(edges + places), first, other, norm, bias, *blocks)

    received = swap_pair(send)
    decoded = pl.pallas_call(
        merge_kernel,
        out_shape=jax.ShapeDtypeStruct((nf * strip * rows, chans), BF16),
        in_specs=[VMEM] * 3,
        out_specs=VMEM,
        compiler_params=PARAMS,
        name="merge",
    )(keep, received, order)
    return decoded.reshape(latent.shape)


def solution(mesh):
    placed = (
        P("tm", "tile", None, None),
        P(None, None, None, "tile", None),
        P(),
        P(),
        P(None, None, None, "tile", None),
        P(),
    )
    return jax.shard_map(
        shards, mesh=mesh, in_specs=placed, out_specs=P("tm", "tile", None, None), check_vma=False
    )
```
